32 devices in a mesh: rep: 16 (over z, y, core), shard: 2 (over x).
Axes of the slice: x: 2, y: 2, z: 4, core: 2. Of those that a mesh axis runs over, the one named last changes fastest.
Arguments:
- inputs: bfloat16 [4096, 1024], P(('rep', 'shard')), may hold values from -6 to 6
- attn_gain: bfloat16 [1024], P('shard'), may hold values from 0.25 to 1.75
- attn_shift: bfloat16 [1024], P('shard'), may hold values from -3 to 3
- feed_gain: bfloat16 [1024], P('shard'), may hold values from 0.25 to 1.75
- feed_shift: bfloat16 [1024], P('shard'), may hold values from -3 to 3
- qkv_weight: bfloat16 [1024, 3072], P(None, 'shard'), may hold values from -0.1875 to 0.1875
- qkv_bias: bfloat16 [3072], P('shard'), may hold values from -3 to 3
- out_weight: bfloat16 [1024, 1024], P(None, 'shard'), may hold values from -0.75 to 0.75
- out_bias: bfloat16 [1024], P('shard'), may hold values from -3 to 3
- up_weight: bfloat16 [1024, 4096], P(None, 'shard'), may hold values from -0.1875 to 0.1875
- up_bias: bfloat16 [4096], P('shard'), may hold values from -3 to 3
- down_weight: bfloat16 [4096, 1024], P('shard'), may hold values from -0.09375 to 0.09375
- down_bias: bfloat16 [1024], P('shard'), may hold values from -3 to 3
- cotangent: bfloat16 [4096, 1024], P(('rep', 'shard')), may hold values from -6 to 6
Outputs:
- outputs: bfloat16 [4096, 1024], P(('rep', 'shard'))
- input_grad: float32 [4096, 1024], P(('rep', 'shard'))
- grad_attn_gain: float32 [1024], P('shard')
- grad_attn_shift: float32 [1024], P('shard')
- grad_feed_gain: float32 [1024], P('shard')
- grad_feed_shift: float32 [1024], P('shard')
- grad_qkv_weight: float32 [1024, 3072], P(None, 'shard')
- grad_qkv_bias: float32 [3072], P('shard')
- grad_out_weight: float32 [1024, 1024], P(None, 'shard')
- grad_out_bias: float32 [1024], P('shard')
- grad_up_weight: float32 [1024, 4096], P(None, 'shard')
- grad_up_bias: float32 [4096], P('shard')
- grad_down_weight: float32 [4096, 1024], P('shard')
- grad_down_bias: float32 [1024], P('shard')
The draws below stay inside these ranges and needn't reach their ends.
All inputs are finite; a program needn't handle non-finite values.
Results may differ from the reference program's by a relative error of at most 0.012.
Values may be sent and summed in bfloat16 or wider, within the bound.
No kernel may reach another device: no remote copies, remote signals or barrier semaphores. Data moves between devices by JAX's collectives and lax.ppermute only.
A program may use at most 192 MiB of HBM per device.

```python
import math
import jax
import jax.numpy as jnp
from jax import lax

D = 1024
H = 16
HD = 64
ROT = 16
FF = 4096
LEN = 128
TOKENS = 4096


def spiked(entries, own_key, source, target, blocks, factor):
    owner, partner = [(jnp.arange(entries.shape[dim]) // (entries.shape[dim] // blocks)).reshape([-1 if axis == dim else 1 for axis in range(entries.ndim)]) for dim in (source, target)]
    chosen = jax.random.permutation(own_key, blocks)[partner]
    strong = (owner == chosen) | (owner == (partner + blocks // 2) % blocks)
    return jnp.where(strong, factor * entries, entries)


def levels(stream_key, extent, cuts, least, top_value):
    def one(position, parts):
        heights = jax.random.uniform(jax.random.fold_in(jax.random.fold_in(stream_key, 6), position), (parts,), jnp.float32, least / len(cuts), top_value / len(cuts))
        return jnp.repeat(jnp.exp(heights), extent[position] // parts).reshape((-1,) + (1,) * (len(extent) - position - 1))

    loudness = one(*cuts[0])
    for cut in cuts[1:]:
        loudness = loudness * one(*cut)
    return loudness


def bell_draw(rng, dims, spread, reach, shards=(), dtype=jnp.bfloat16):
    level = levels(rng, dims, shards, -0.22, 0.18) if shards else 1.0
    values = jax.random.normal(rng, dims, jnp.float32) * spread * level
    return jnp.minimum(jnp.maximum(values, -reach), reach).astype(dtype)


def gaussian_with(stream_key, dims, width, bound, cuts, heavy, held_as=jnp.bfloat16):
    entries = width * jax.random.normal(stream_key, dims, jnp.float32)
    if cuts:
        entries = entries * levels(stream_key, dims, cuts, -0.22, 0.18)
    return jnp.clip(spiked(entries, jax.random.fold_in(stream_key, 3), *heavy), -bound, bound).astype(held_as)


def setup_inputs(seed: int = 0) -> dict:
    key_of = jax.random.split(jax.random.key(seed), 15)
    return {
        "inputs": bell_draw(key_of[0], (TOKENS, D), 1.0, 6.0, ((0, 32),)),
        "attn_gain": jnp.clip(1.0 + 0.15 * jax.random.normal(key_of[1], (D,), jnp.float32), 0.25, 1.75).astype(jnp.bfloat16),
        "attn_shift": bell_draw(key_of[2], (D,), 0.5, 3.0, ((0, 2),)),
        "feed_gain": jnp.clip(1.0 + 0.15 * jax.random.normal(key_of[3], (D,), jnp.float32), 0.25, 1.75).astype(jnp.bfloat16),
        "feed_shift": bell_draw(key_of[4], (D,), 0.5, 3.0, ((0, 2),)),
        "qkv_weight": bell_draw(key_of[5], (D, 3 * D), D ** -0.5, 0.1875, ((1, 2),)),
        "qkv_bias": bell_draw(key_of[6], (3 * D,), 0.5, 3.0, ((0, 2),)),
        "out_weight": bell_draw(key_of[7], (D, D), (D // 16) ** -0.5, 0.75, ((1, 2),)),
        "out_bias": bell_draw(key_of[8], (D,), 0.5, 3.0, ((0, 2),)),
        "up_weight": bell_draw(key_of[9], (D, FF), D ** -0.5, 0.1875, ((1, 2),)),
        "up_bias": bell_draw(key_of[10], (FF,), 0.5, 3.0, ((0, 2),)),
        "down_weight": bell_draw(key_of[11], (FF, D), FF ** -0.5, 0.09375, ((0, 2),)),
        "down_bias": bell_draw(key_of[12], (D,), 0.5, 3.0, ((0, 2),)),
        "cotangent": gaussian_with(key_of[13], (TOKENS, D), 1.0, 6.0, ((0, 32),), (0, 1, 32, 2.75)),
    }


norm_eps = 1e-05
base_freq = 10000.0

def round_trip(values):
    return lax.optimization_barrier(values.astype(jnp.bfloat16)).astype(jnp.float32)

def rotary_tables(length, rotary_dims):
    half_dims = rotary_dims // 2
    positions = jnp.arange(length).astype(jnp.float32)
    inverse = jnp.exp(jnp.arange(half_dims).astype(jnp.float32) * (-2.0 * math.log(base_freq) / rotary_dims))
    angles = positions[:, None] * inverse[None, :]
    return (jnp.cos(angles), jnp.sin(angles))

def rotate(values, cosine, sine_table, rotary_dims, direction):
    half_dims = rotary_dims // 2
    lower_half = values[..., :half_dims]
    upper_half = values[..., half_dims:rotary_dims]
    cosine_row = cosine[:, None, :]
    sine_row = sine_table[:, None, :] * direction
    return jnp.concatenate([lower_half * cosine_row - upper_half * sine_row, upper_half * cosine_row + lower_half * sine_row, values[..., rotary_dims:]], axis=-1)

def gelu_slope(preact):
    normal_cdf = 0.5 * (1.0 + jax.scipy.special.erf(preact * (1.0 / math.sqrt(2.0))))
    return normal_cdf + preact * jnp.exp(-0.5 * preact * preact) * (1.0 / math.sqrt(2.0 * math.pi))

def sequences_pass(x_rows, dy_rows, weights):
    attn_gain, attn_shift, feed_gain, feed_shift, qkv_weight, qkv_bias, out_weight, out_bias, up_weight, up_bias, down_weight, down_bias = weights
    total_rows = x_rows.shape[0]
    seq_count = total_rows // LEN
    gain_one = attn_gain.astype(jnp.float32)
    gain_two = feed_gain.astype(jnp.float32)
    resid = x_rows.astype(jnp.float32)
    row_mean = lax.optimization_barrier(jnp.mean(resid, -1, keepdims=True))
    centered = resid - row_mean
    inv_std = lax.rsqrt(lax.optimization_barrier(jnp.mean(centered * centered, -1, keepdims=True)) + norm_eps)
    normed = centered * inv_std
    attn_in = (normed * gain_one + attn_shift.astype(jnp.float32)).astype(jnp.bfloat16)
    feed_in = (normed * gain_two + feed_shift.astype(jnp.float32)).astype(jnp.bfloat16)
    projected = jnp.dot(attn_in, qkv_weight, preferred_element_type=jnp.float32) + qkv_bias.astype(jnp.float32)
    projected = projected.reshape(seq_count, LEN, 3, H, HD)
    cosine, sine_table = rotary_tables(LEN, ROT)
    query_f = round_trip(rotate(projected[:, :, 0], cosine, sine_table, ROT, 1.0))
    keys_f = round_trip(rotate(projected[:, :, 1], cosine, sine_table, ROT, 1.0))
    values_f = round_trip(projected[:, :, 2])
    score_scale = 1.0 / math.sqrt(HD)
    causal = jnp.arange(LEN)[:, None] >= jnp.arange(LEN)[None, :]
    scores = jnp.einsum('bqhd,bkhd->bhqk', query_f, keys_f) * score_scale
    scores = jnp.where(causal[None, None], scores, -jnp.inf)
    row_max = lax.optimization_barrier(jnp.max(scores, -1, keepdims=True))
    log_total = row_max + jnp.log(lax.optimization_barrier(jnp.sum(jnp.exp(scores - row_max), -1, keepdims=True)))
    probs_f = jnp.exp(scores - log_total)
    probs_b = round_trip(probs_f)
    attended = jnp.einsum('bhqk,bkhd->bqhd', probs_b, values_f).astype(jnp.bfloat16).reshape(total_rows, D)
    attn_out = jnp.dot(attended, out_weight, preferred_element_type=jnp.float32) + out_bias.astype(jnp.float32)
    preact = jnp.dot(feed_in, up_weight, preferred_element_type=jnp.float32) + up_bias.astype(jnp.float32)
    hidden = jax.nn.gelu(preact, approximate=False).astype(jnp.bfloat16)
    feed_out = jnp.dot(hidden, down_weight, preferred_element_type=jnp.float32) + down_bias.astype(jnp.float32)
    outputs = (resid + attn_out + feed_out).astype(jnp.bfloat16)
    grad_top = dy_rows.astype(jnp.float32)
    grad_bias = lax.optimization_barrier(jnp.sum(grad_top, 0))
    grad_out_w = jnp.dot(attended.T, dy_rows, preferred_element_type=jnp.float32)
    grad_attended = jnp.dot(dy_rows, out_weight.T, preferred_element_type=jnp.float32).astype(jnp.bfloat16)
    grad_down = jnp.dot(hidden.T, dy_rows, preferred_element_type=jnp.float32)
    grad_preact = jnp.dot(dy_rows, down_weight.T, preferred_element_type=jnp.float32) * gelu_slope(preact)
    grad_up_b = lax.optimization_barrier(jnp.sum(grad_preact, 0))
    grad_preact_b = grad_preact.astype(jnp.bfloat16)
    grad_up = jnp.dot(feed_in.T, grad_preact_b, preferred_element_type=jnp.float32)
    grad_feed_in = jnp.dot(grad_preact_b, up_weight.T, preferred_element_type=jnp.float32)
    grad_att_f = grad_attended.astype(jnp.float32).reshape(seq_count, LEN, H, HD)
    grad_values = jnp.einsum('bhqk,bqhd->bkhd', probs_b, grad_att_f)
    grad_probs = jnp.einsum('bqhd,bkhd->bhqk', grad_att_f, values_f)
    grad_scores = probs_f * (grad_probs - lax.optimization_barrier(jnp.sum(probs_f * grad_probs, -1, keepdims=True))) * score_scale
    grad_scores_f = round_trip(grad_scores)
    grad_qrot = jnp.einsum('bhqk,bkhd->bqhd', grad_scores_f, keys_f)
    grad_krot = jnp.einsum('bhqk,bqhd->bkhd', grad_scores_f, query_f)
    grad_query = rotate(grad_qrot, cosine, sine_table, ROT, -1.0)
    grad_keys = rotate(grad_krot, cosine, sine_table, ROT, -1.0)
    grad_proj = jnp.stack([grad_query, grad_keys, grad_values], axis=2).reshape(total_rows, 3 * D)
    grad_qkv_b = lax.optimization_barrier(jnp.sum(grad_proj, 0))
    grad_proj_b = grad_proj.astype(jnp.bfloat16)
    grad_qkv = jnp.dot(attn_in.T, grad_proj_b, preferred_element_type=jnp.float32)
    grad_attn_in = jnp.dot(grad_proj_b, qkv_weight.T, preferred_element_type=jnp.float32)
    grad_gain_one = lax.optimization_barrier(jnp.sum(grad_attn_in * normed, 0))
    grad_shift_one = lax.optimization_barrier(jnp.sum(grad_attn_in, 0))
    grad_gain_two = lax.optimization_barrier(jnp.sum(grad_feed_in * normed, 0))
    grad_shift_two = lax.optimization_barrier(jnp.sum(grad_feed_in, 0))
    grad_normed = grad_attn_in * gain_one + grad_feed_in * gain_two
    input_grad = grad_top + inv_std * (grad_normed - lax.optimization_barrier(jnp.mean(grad_normed, -1, keepdims=True)) - normed * lax.optimization_barrier(jnp.mean(grad_normed * normed, -1, keepdims=True)))
    grads = (grad_gain_one, grad_shift_one, grad_gain_two, grad_shift_two, grad_qkv, grad_qkv_b, grad_out_w, grad_bias, grad_up, grad_up_b, grad_down, grad_bias)
    return (outputs, input_grad, grads)

def reference(inputs, attn_gain, attn_shift, feed_gain, feed_shift, qkv_weight, qkv_bias, out_weight, out_bias, up_weight, up_bias, down_weight, down_bias, cotangent):
    seqs_block = math.gcd(TOKENS // LEN, max(1, 4096 // LEN))
    block_rows = seqs_block * LEN
    block_count = TOKENS // block_rows
    weights = (attn_gain, attn_shift, feed_gain, feed_shift, qkv_weight, qkv_bias, out_weight, out_bias, up_weight, up_bias, down_weight, down_bias)
    x_blocks = inputs.reshape(block_count, block_rows, D)
    dy_blocks = cotangent.reshape(block_count, block_rows, D)
    initial = tuple((jnp.zeros(w.shape, jnp.float32) for w in weights))

    def step_block(carry, pair):
        outputs, input_grad, grads = sequences_pass(pair[0], pair[1], weights)
        return (tuple((a + b for a, b in zip(carry, grads))), (outputs, input_grad))
    grads, (out_blocks, grad_blocks) = lax.scan(step_block, initial, (x_blocks, dy_blocks))
    return (out_blocks.reshape(TOKENS, D), grad_blocks.reshape(TOKENS, D), grads[0], grads[1], grads[2], grads[3], grads[4], grads[5], grads[6], grads[7], grads[8], grads[9], grads[10], grads[11])
```

```python
import math

import jax
import jax.numpy as jnp
from jax import lax
from jax.sharding import PartitionSpec as P

D = 1024
H = 16
HD = 64
ROT = 16


norm_eps = 1e-05
base_freq = 10000.0


def rotary_tables(length, rotary_dims):
    half_dims = rotary_dims // 2
    positions = jnp.arange(length).astype(jnp.float32)
    inverse = jnp.exp(
        jnp.arange(half_dims).astype(jnp.float32) * (-2.0 * math.log(base_freq) / rotary_dims)
    )
    angles = positions[:, None] * inverse[None, :]
    return (jnp.cos(angles), jnp.sin(angles))


def rotate(values, cosine, sine_table, rotary_dims, direction):
    half_dims = rotary_dims // 2
    lower_half = values[..., :half_dims]
    upper_half = values[..., half_dims:rotary_dims]
    cosine_row = cosine[:, None, :]
    sine_row = sine_table[:, None, :] * direction
    return jnp.concatenate(
        [
            lower_half * cosine_row - upper_half * sine_row,
            upper_half * cosine_row + lower_half * sine_row,
            values[..., rotary_dims:],
        ],
        axis=-1,
    )


def gelu_slope(preact):
    normal_cdf = 0.5 * (1.0 + jax.scipy.special.erf(preact * (1.0 / math.sqrt(2.0))))
    return normal_cdf + preact * jnp.exp(-0.5 * preact * preact) * (1.0 / math.sqrt(2.0 * math.pi))


def body(
    inputs,
    attn_gain,
    attn_shift,
    feed_gain,
    feed_shift,
    qkv_weight,
    qkv_bias,
    out_weight,
    out_bias,
    up_weight,
    up_bias,
    down_weight,
    down_bias,
    cotangent,
):
    (
        gain_one,
        shift_one,
        gain_two,
        shift_two,
        out_bias_all,
        down_bias_all,
        qkv_all,
        qkv_bias_all,
        out_all,
    ) = (
        lax.all_gather(attn_gain, "shard", axis=0, tiled=True),
        lax.all_gather(attn_shift, "shard", axis=0, tiled=True),
        lax.all_gather(feed_gain, "shard", axis=0, tiled=True),
        lax.all_gather(feed_shift, "shard", axis=0, tiled=True),
        lax.all_gather(out_bias, "shard", axis=0, tiled=True),
        lax.all_gather(down_bias, "shard", axis=0, tiled=True),
        lax.all_gather(qkv_weight, "shard", axis=1, tiled=True),
        lax.all_gather(qkv_bias, "shard", axis=0, tiled=True),
        lax.all_gather(out_weight, "shard", axis=1, tiled=True),
    )
    gain_one = gain_one.astype(jnp.float32)
    gain_two = gain_two.astype(jnp.float32)
    length = inputs.shape[0]
    resid = inputs.astype(jnp.float32)
    row_mean = jnp.mean(resid, -1, keepdims=True)
    centered = resid - row_mean
    inv_std = lax.rsqrt(jnp.mean(centered * centered, -1, keepdims=True) + norm_eps)
    normed = centered * inv_std
    attn_in = (normed * gain_one + shift_one.astype(jnp.float32)).astype(jnp.bfloat16)
    feed_in = (normed * gain_two + shift_two.astype(jnp.float32)).astype(jnp.bfloat16)
    projected = jnp.dot(attn_in, qkv_all, preferred_element_type=jnp.float32) + qkv_bias_all.astype(
        jnp.float32
    )
    projected = projected.reshape(length, 3, H, HD)
    cosine, sine_table = rotary_tables(length, ROT)
    query_rot = rotate(projected[:, 0], cosine, sine_table, ROT, 1.0).astype(jnp.bfloat16)
    keys_rot = rotate(projected[:, 1], cosine, sine_table, ROT, 1.0).astype(jnp.bfloat16)
    values_b = projected[:, 2].astype(jnp.bfloat16)
    score_scale = 1.0 / math.sqrt(HD)
    row_block = min(512, length)
    block_count = length // row_block
    key_positions = jnp.arange(length)

    def block_scores(row_start, q_rows):
        scores = (
            jnp.einsum("qhd,khd->hqk", q_rows, keys_rot, preferred_element_type=jnp.float32)
            * score_scale
        )
        causal = (row_start + jnp.arange(row_block))[:, None] >= key_positions[None, :]
        return jnp.where(causal[None], scores, -jnp.inf)

    def forward_block(block_index):
        row_start = block_index * row_block
        scores = block_scores(row_start, query_rot)
        row_max = jnp.max(scores, -1, keepdims=True)
        log_total = row_max + jnp.log(jnp.sum(jnp.exp(scores - row_max), -1, keepdims=True))
        attn_probs = jnp.exp(scores - log_total).astype(jnp.bfloat16)
        block_out = jnp.einsum(
            "hqk,khd->qhd", attn_probs, values_b, preferred_element_type=jnp.float32
        )
        return (block_out.astype(jnp.bfloat16), log_total)

    attended, log_totals = lax.map(forward_block, jnp.arange(block_count))
    attended = attended.reshape(length, D)
    attn_out = jnp.dot(attended, out_all, preferred_element_type=jnp.float32) + out_bias_all.astype(
        jnp.float32
    )
    group_in = lax.all_gather(feed_in, "shard", axis=0, tiled=True)
    preact = jnp.dot(group_in, up_weight, preferred_element_type=jnp.float32) + up_bias.astype(
        jnp.float32
    )
    hidden = jax.nn.gelu(preact, approximate=False).astype(jnp.bfloat16)
    rows_in = hidden
    feed_out = lax.psum_scatter(
        jnp.dot(rows_in, down_weight, preferred_element_type=jnp.float32),
        "shard",
        scatter_dimension=0,
        tiled=True,
    ) + down_bias_all.astype(jnp.float32)
    outputs = (resid + attn_out + feed_out).astype(jnp.bfloat16)
    grad_top = cotangent.astype(jnp.float32)
    attn_group, attended_group, out_back = (
        lax.all_gather(attn_in, "shard", axis=0, tiled=True),
        lax.all_gather(attended, "shard", axis=0, tiled=True),
        lax.all_gather(out_weight, "shard", axis=1, tiled=True),
    )
    grad_cols = lax.all_to_all(cotangent, "shard", split_axis=1, concat_axis=0, tiled=True)
    grad_bias = jnp.sum(grad_cols.astype(jnp.float32), 0)
    grad_out_w = jnp.dot(attended_group.T, grad_cols, preferred_element_type=jnp.float32)
    grad_attended = (
        jnp.dot(cotangent, out_back.T, preferred_element_type=jnp.float32)
        .astype(jnp.bfloat16)
        .reshape(length, H, HD)
    )
    group_grad = lax.all_gather(cotangent, "shard", axis=0, tiled=True)
    grad_down = jnp.dot(hidden.T, group_grad, preferred_element_type=jnp.float32)
    grad_preact = jnp.dot(
        group_grad, down_weight.T, preferred_element_type=jnp.float32
    ) * gelu_slope(preact)
    grad_up_b = jnp.sum(grad_preact, 0)
    grad_preact_b = grad_preact.astype(jnp.bfloat16)
    grad_up = jnp.dot(group_in.T, grad_preact_b, preferred_element_type=jnp.float32)
    rows_in = grad_preact_b
    grad_feed_in = lax.psum_scatter(
        jnp.dot(rows_in, up_weight.T, preferred_element_type=jnp.float32),
        "shard",
        scatter_dimension=0,
        tiled=True,
    )

    def backward_block(carry, block_index):
        grad_keys, grad_values = carry
        row_start = block_index * row_block
        scores = block_scores(row_start, query_rot)
        probs_f = jnp.exp(scores - log_totals[block_index])
        probs_b = probs_f.astype(jnp.bfloat16)
        grad_values = grad_values + jnp.einsum(
            "hqk,qhd->khd", probs_b, grad_attended, preferred_element_type=jnp.float32
        )
        grad_probs = jnp.einsum(
            "qhd,khd->hqk", grad_attended, values_b, preferred_element_type=jnp.float32
        )
        grad_scores = (
            probs_f * (grad_probs - jnp.sum(probs_f * grad_probs, -1, keepdims=True)) * score_scale
        )
        grad_scores_b = grad_scores.astype(jnp.bfloat16)
        grad_qrot = jnp.einsum(
            "hqk,khd->qhd", grad_scores_b, keys_rot, preferred_element_type=jnp.float32
        )
        grad_keys = grad_keys + jnp.einsum(
            "hqk,qhd->khd", grad_scores_b, query_rot, preferred_element_type=jnp.float32
        )
        return ((grad_keys, grad_values), grad_qrot)

    empty_heads = jnp.zeros((length, H, HD), jnp.float32)
    (grad_krot, grad_values), grad_qrot = lax.scan(
        backward_block, (empty_heads, empty_heads), jnp.arange(block_count)
    )
    grad_qrot = grad_qrot.reshape(length, H, HD)
    grad_query = rotate(grad_qrot, cosine, sine_table, ROT, -1.0)
    grad_keys = rotate(grad_krot, cosine, sine_table, ROT, -1.0)
    grad_proj = jnp.stack([grad_query, grad_keys, grad_values], axis=1).reshape(length, 3 * D)
    grad_qkv_b = jnp.sum(grad_proj, 0)
    grad_proj_b = grad_proj.astype(jnp.bfloat16)
    proj_cols = lax.all_to_all(grad_proj_b, "shard", split_axis=1, concat_axis=0, tiled=True)
    grad_qkv = jnp.dot(attn_group.T, proj_cols, preferred_element_type=jnp.float32)
    rows_in = proj_cols
    grad_attn_in = lax.psum_scatter(
        jnp.dot(rows_in, qkv_weight.T, preferred_element_type=jnp.float32),
        "shard",
        scatter_dimension=0,
        tiled=True,
    )
    grad_gain_one = jnp.sum(grad_attn_in * normed, 0)
    grad_shift_one = jnp.sum(grad_attn_in, 0)
    grad_gain_two = jnp.sum(grad_feed_in * normed, 0)
    grad_shift_two = jnp.sum(grad_feed_in, 0)
    grad_normed = grad_attn_in * gain_one + grad_feed_in * gain_two
    input_grad = grad_top + inv_std * (
        grad_normed
        - jnp.mean(grad_normed, -1, keepdims=True)
        - normed * jnp.mean(grad_normed * normed, -1, keepdims=True)
    )
    grad_qkv_b, grad_gain_one, grad_shift_one, grad_gain_two, grad_shift_two = (
        lax.psum_scatter(grad_qkv_b, "shard", scatter_dimension=0, tiled=True),
        lax.psum_scatter(grad_gain_one, "shard", scatter_dimension=0, tiled=True),
        lax.psum_scatter(grad_shift_one, "shard", scatter_dimension=0, tiled=True),
        lax.psum_scatter(grad_gain_two, "shard", scatter_dimension=0, tiled=True),
        lax.psum_scatter(grad_shift_two, "shard", scatter_dimension=0, tiled=True),
    )
    grad_qkv, grad_out_w, grad_up, grad_down = [
        lax.psum(g.astype(jnp.bfloat16), "rep").astype(jnp.float32)
        for g in (grad_qkv, grad_out_w, grad_up, grad_down)
    ]
    vectors = (grad_gain_one, grad_shift_one, grad_gain_two, grad_shift_two, grad_qkv_b, grad_bias, grad_up_b)
    summed = lax.psum(jnp.concatenate(vectors), "rep")
    cuts = []
    start = 0
    for vector in vectors:
        cuts.append(summed[start : start + vector.shape[0]])
        start += vector.shape[0]
    grad_gain_one, grad_shift_one, grad_gain_two, grad_shift_two, grad_qkv_b, grad_bias, grad_up_b = cuts
    return (
        outputs,
        input_grad,
        grad_gain_one,
        grad_shift_one,
        grad_gain_two,
        grad_shift_two,
        grad_qkv,
        grad_qkv_b,
        grad_out_w,
        grad_bias,
        grad_up,
        grad_up_b,
        grad_down,
        grad_bias,
    )


def solution(mesh):
    return jax.shard_map(
        body,
        mesh=mesh,
        in_specs=(
            P(("rep", "shard"), None),
            P("shard"),
            P("shard"),
            P("shard"),
            P("shard"),
            P(None, "shard"),
            P("shard"),
            P(None, "shard"),
            P("shard"),
            P(None, "shard"),
            P("shard"),
            P("shard", None),
            P("shard"),
            P(("rep", "shard"), None),
        ),
        out_specs=(
            P(("rep", "shard"), None),
            P(("rep", "shard"), None),
            P("shard"),
            P("shard"),
            P("shard"),
            P("shard"),
            P(None, "shard"),
            P("shard"),
            P(None, "shard"),
            P("shard"),
            P(None, "shard"),
            P("shard"),
            P("shard", None),
            P("shard"),
        ),
        check_vma=False,
    )
```
